32 devices in a mesh: prow: 8 (over z, y), pcol: 4 (over x, core).
Axes of the slice: x: 2, y: 2, z: 4, core: 2. Of those that a mesh axis runs over, the one named last changes fastest.
Arguments:
- matrix: float32 [2048, 2048], P('prow', 'pcol'), as said below
Outputs:
- complement: float32 [2048, 2048], P('prow', 'pcol')
- panel_columns: float32 [2048, 512], P(('prow', 'pcol'))
- pivot_values: float32 [512], replicated
Inputs may be any that keep to these rules, and one draw needn't show every extreme that they name: matrix is symmetric and positive definite, with its smallest eigenvalue above a six-hundredth of its largest diagonal entry.
All inputs are finite; a program needn't handle non-finite values.
Results may differ from the reference program's by a relative error of at most 0.00014.
Values sent between devices are 32-bit elements; how exact they have to be, the bound alone decides.
A program may use at most 128 MiB of HBM per device.

```python
import math
import jax
import jax.numpy as jnp
from jax import lax

NB = 256
PANELS = 2
ORDER = 2048


def draw_matrix(key, part):
    base = jax.random.fold_in(key, 17)
    first_key, second_key, third_key = jax.random.split(base, 3)
    points = jax.random.uniform(first_key, (ORDER, 3), jnp.float32, 0.0, 1.0)
    angles = jax.random.uniform(second_key, (ORDER,), jnp.float32, -math.pi, math.pi)
    rescale = jnp.exp(jax.random.uniform(third_key, (ORDER,), jnp.float32, math.log(0.6), math.log(1.6)))
    reach = (0.764 / (PANELS * NB)) ** (1.0 / 3.0)
    first_gap = points[:, None, 0] - points[None, :, 0]
    second_gap = points[:, None, 1] - points[None, :, 1]
    third_gap = points[:, None, 2] - points[None, :, 2]
    distance = jnp.sqrt(first_gap * first_gap + second_gap * second_gap + third_gap * third_gap)
    kernel = jnp.exp(-distance / reach)
    cosine = jnp.cos(angles)
    sine = jnp.sin(angles)
    phase = cosine[:, None] * cosine[None, :] + sine[:, None] * sine[None, :]
    index_rows = jnp.arange(ORDER).astype(jnp.int32)
    lifted = jnp.where(index_rows[:, None] == index_rows[None, :], jnp.float32(0.25), jnp.float32(0.0))
    core = kernel * phase + lifted
    outer = rescale[:, None] * rescale[None, :]
    return (core * outer).astype(jnp.float32)


def setup_inputs(seed: int = 0) -> dict:
    splits = jax.random.split(jax.random.key(seed), 2)
    matrix = draw_matrix(jax.random.fold_in(splits[1], 71), 0)
    return dict(matrix=matrix)


def reference(matrix):
    current = matrix
    position = jnp.arange(ORDER).astype(jnp.int32)
    column_list = []
    pivot_list = []
    for panel in range(PANELS):
        first = panel * NB
        diagonal = current[first:first + NB, first:first + NB]
        cholesky_factor = jnp.linalg.cholesky(diagonal)
        scaling = jnp.diagonal(cholesky_factor)
        identity = jnp.eye(NB, dtype=current.dtype)
        inverse = jax.scipy.linalg.solve_triangular(cholesky_factor, identity, lower=True)
        projected = jnp.dot(current[:, first:first + NB], inverse.T, precision=lax.Precision.HIGHEST)
        factored = projected * scaling
        pivot = scaling * scaling
        weighed = factored / pivot
        current = current - jnp.dot(weighed, factored.T, precision=lax.Precision.HIGHEST)
        retained = position >= first + NB
        current = jnp.where(retained[:, None] & retained[None, :], current, jnp.zeros_like(current))
        column_list.append(factored)
        pivot_list.append(pivot)
    return (current, jnp.concatenate(column_list, axis=1), jnp.concatenate(pivot_list))
```

```python
import functools

import jax
import jax.numpy as jnp
from jax import lax
from jax.experimental import pallas as pl
from jax.experimental.pallas import tpu as pltpu
from jax.sharding import PartitionSpec as P

NB = 256
PANELS = 2
BLOCK = 128
SUB = 8
CHUNKS = 4

HIGHEST = lax.Precision.HIGHEST
MESH = pl.DeviceIdType.MESH
VMEM = pltpu.VMEM


def matmul(left, right):
    return lax.dot_general(
        left, right, (((1,), (0,)), ((), ())),
        precision=HIGHEST, preferred_element_type=jnp.float32,
    )


def against(left, right):
    return lax.dot_general(
        left, right, (((1,), (1,)), ((), ())),
        precision=HIGHEST, preferred_element_type=jnp.float32,
    )


def exchange(rows, cols, chain, a_ref, col_ref, diag_ref, row_ref, *sems):
    zs, zr, ys, yr, es, er, fs, fr, rs, rr, local = sems
    r, c = lax.axis_index("prow"), lax.axis_index("pcol")
    height = a_ref.shape[0]
    piece = lax.rem(r, chain)
    other = chain - 1 - piece
    partner = r - piece + other
    step = height // CHUNKS
    has_next, has_prev = r + chain < rows, r >= chain
    even = lax.rem(c, 2) == 0
    mate = c + 1 - 2 * lax.rem(c, 2)
    has_right, has_left = even & (c + 2 < cols), even & (c >= 2)
    gets = c > 0

    barrier = pltpu.get_barrier_semaphore()

    def greet(dev):
        pl.semaphore_signal(barrier, inc=1, device_id=dev, device_id_type=MESH)

    greet((partner, c))
    greet((r, mate))
    pl.when(has_next)(lambda: greet((r + chain, c)))
    pl.when(has_prev)(lambda: greet((r - chain, c)))
    pl.when(has_right)(lambda: greet((r, c + 2)))
    pl.when(has_left)(lambda: greet((r, c - 2)))
    one = lambda flag: flag.astype(jnp.int32)
    pl.semaphore_wait(
        barrier, 2 + one(has_next) + one(has_prev) + one(has_right) + one(has_left)
    )

    def remote(ref, source, target, send, recv, dev):
        return pltpu.make_async_remote_copy(
            src_ref=source, dst_ref=ref.at[target] if target is not None else ref,
            send_sem=send, recv_sem=recv, device_id=dev, device_id_type=MESH,
        )

    def part(block, k):
        return pl.ds(pl.multiple_of(block * height + k * step, step), step)

    def z_copy(k):
        s = part(piece, k)
        return remote(col_ref, col_ref.at[s], s, zs.at[k], zr.at[k], (r + chain, c))

    def y_copy(k, block):
        s = part(block, k)
        return remote(col_ref, col_ref.at[s], s, ys.at[k], yr.at[k], (partner, c))

    def mate_copy(source, block, k, q):
        s = part(block, k)
        return remote(diag_ref, source.at[s], s, es.at[q], er.at[q], (r, c + 1))

    def right_copy(source, block, k, q):
        s = part(block, k)
        return remote(diag_ref, source.at[s], s, fs.at[q], er.at[q], (r, c + 2))

    def row_mate(source):
        return remote(row_ref, source, None, rs.at[0], rr.at[0], (r, c + 1))

    def row_right(source):
        return remote(row_ref, source, None, rs.at[1], rr.at[0], (r, c + 2))

    @pl.when(jnp.logical_not(has_prev))
    def _():
        copy = pltpu.make_async_copy(
            a_ref, col_ref.at[pl.ds(pl.multiple_of(piece * height, height), height)], local.at[0]
        )
        copy.start()
        copy.wait()

    def spread(source, block, k, q):
        pl.when(even)(lambda: mate_copy(source, block, k, q).start())
        pl.when(has_right)(lambda: right_copy(source, block, k, q).start())

    for k in range(CHUNKS):
        pl.when(has_prev)(lambda: z_copy(k).wait_recv())
        pl.when(has_next)(lambda: z_copy(k).start())
        y_copy(k, piece).start()
        pl.when(c == 0)(lambda: spread(col_ref, piece, k, k))
        if k >= 1:
            y_copy(k - 1, other).wait_recv()
            pl.when(c == 0)(lambda: spread(col_ref, other, k - 1, CHUNKS + k - 1))

        @pl.when(gets)
        def _():
            if k >= 1:
                mate_copy(diag_ref, piece, k - 1, k - 1).wait_recv()
                pl.when(even)(lambda: spread(diag_ref, piece, k - 1, k - 1))
            if k >= 2:
                q = CHUNKS + k - 2
                mate_copy(diag_ref, other, k - 2, q).wait_recv()
                pl.when(even)(lambda: spread(diag_ref, other, k - 2, q))

    k = CHUNKS - 1
    y_copy(k, other).wait_recv()

    @pl.when(c == 0)
    def _():
        spread(col_ref, other, k, CHUNKS + k)
        row_mate(a_ref).start()
        pl.when(has_right)(lambda: row_right(a_ref).start())
        copies = [
            pltpu.make_async_copy(a_ref, row_ref, local.at[1]),
            pltpu.make_async_copy(col_ref, diag_ref, local.at[2]),
        ]
        for copy in copies:
            copy.start()
        for copy in copies:
            copy.wait()

    @pl.when(gets)
    def _():
        for block, k, q in (
            (piece, CHUNKS - 1, CHUNKS - 1),
            (other, CHUNKS - 2, 2 * CHUNKS - 2),
            (other, CHUNKS - 1, 2 * CHUNKS - 1),
        ):
            mate_copy(diag_ref, block, k, q).wait_recv()
            pl.when(even)(lambda: spread(diag_ref, block, k, q))
        row_mate(row_ref).wait_recv()

        @pl.when(even)
        def _():
            row_mate(row_ref).start()
            pl.when(has_right)(lambda: row_right(row_ref).start())

    for k in range(CHUNKS):
        pl.when(has_next)(lambda: z_copy(k).wait_send())
        y_copy(k, piece).wait_send()
    for q in range(2 * CHUNKS):
        block, k = (piece, q) if q < CHUNKS else (other, q - CHUNKS)
        pl.when(even)(lambda: mate_copy(diag_ref, block, k, q).wait_send())
        pl.when(has_right)(lambda: right_copy(diag_ref, block, k, q).wait_send())
    pl.when(even)(lambda: row_mate(row_ref).wait_send())
    pl.when(has_right)(lambda: row_right(row_ref).wait_send())


def eliminate(block):
    groups = BLOCK // SUB
    shape = (SUB, BLOCK)
    lane = lax.broadcasted_iota(jnp.int32, shape, 1)
    sub = lax.broadcasted_iota(jnp.int32, shape, 0)
    zero = jnp.zeros(shape, jnp.float32)
    rows = [block[w * SUB : (w + 1) * SUB, :] for w in range(groups)]
    pivots = zero
    spread = lambda x, t: jnp.broadcast_to(x[t : t + 1, :], shape)
    for v in range(groups):
        first = v * SUB
        column = {
            w: [
                jnp.broadcast_to(rows[w][:, first + t : first + t + 1], shape)
                for t in range(SUB)
            ]
            for w in range(v, groups)
        }
        inside = (lane >= first) & (lane < first + SUB)
        identity = jnp.where(lane == sub + first, 1.0, 0.0).astype(jnp.float32)
        rows[v] = jnp.where(inside, identity, rows[v])
        for w in range(v + 1, groups):
            rows[w] = jnp.where(inside, zero, rows[w])
        for t in range(SUB):
            own = column[v]
            pivot = spread(own[t], t)
            inverse = 1.0 / pivot
            pivots = jnp.where(lane == first + t, pivot, pivots)
            entries = {u: spread(own[u], t) for u in range(t + 1, SUB)}
            pivot_row = spread(rows[v], t)
            below = jnp.where(sub > t, own[t], zero)
            for u in range(t + 1, SUB):
                own[u] = own[u] - (below * entries[u]) * inverse
            rows[v] = rows[v] - (below * pivot_row) * inverse
            for w in range(v + 1, groups):
                weight = column[w][t] * inverse
                for u in range(t + 1, SUB):
                    column[w][u] = column[w][u] - weight * entries[u]
                rows[w] = rows[w] - weight * pivot_row
        rows[v] = jnp.where(lane < first + SUB, rows[v], zero)
    return jnp.concatenate(rows, axis=0), pivots[0:1, :]


def solve(a_ref, col_ref, diag_ref, row_ref, out_ref, panel_ref, pivot_ref, work, held):
    r, c = lax.axis_index("prow"), lax.axis_index("pcol")
    depth = diag_ref.shape[0]
    height, width = a_ref.shape
    count = depth // BLOCK
    work[...] = diag_ref[...]
    for b in range(count):
        here = slice(b * BLOCK, (b + 1) * BLOCK)
        inverse, pivots = eliminate(work[here, here])
        pivot_ref[:, here] = pivots
        if b:
            left = matmul(inverse, work[here, : b * BLOCK])
            work[here, : b * BLOCK] = left
        if b + 1 < count:
            after = slice((b + 1) * BLOCK, depth)
            right = matmul(inverse, work[here, after])
            lower = against(work[after, here], inverse) / pivots
            work[after, after] = work[after, after] - matmul(lower, right)
            if b:
                work[after, : b * BLOCK] = work[after, : b * BLOCK] - matmul(lower, left)
            work[after, here] = -matmul(lower, inverse)
        work[here, here] = inverse
        if b + 1 < count:
            work[here, after] = jnp.zeros((BLOCK, depth - (b + 1) * BLOCK), jnp.float32)
    factor = against(row_ref[...], work[...])
    partner = matmul(work[...], col_ref[...])
    weighed = factor / pivot_ref[...]
    update = a_ref[...] - matmul(weighed, partner)
    grow = r * height + lax.broadcasted_iota(jnp.int32, update.shape, 0)
    gcol = c * width + lax.broadcasted_iota(jnp.int32, update.shape, 1)
    out_ref[...] = jnp.where((grow >= depth) & (gcol >= depth), update, 0.0)
    grow = r * height + lax.broadcasted_iota(jnp.int32, factor.shape, 0)
    panel = lax.broadcasted_iota(jnp.int32, factor.shape, 1) // NB
    held[...] = jnp.where(grow >= panel * NB, factor, 0.0)
    portion = panel_ref.shape[0]
    panel_ref[...] = held[pl.ds(pl.multiple_of(c * portion, portion), portion), :]


def on_device(rows, cols, matrix):
    height, width = matrix.shape
    depth = NB * PANELS
    chain = depth // height
    f32 = jnp.float32
    spec = pl.BlockSpec(memory_space=VMEM)
    dma = pltpu.SemaphoreType.DMA
    col, diag, row = pl.pallas_call(
        functools.partial(exchange, rows, cols, chain),
        out_shape=[
            jax.ShapeDtypeStruct((depth, width), f32),
            jax.ShapeDtypeStruct((depth, depth), f32),
            jax.ShapeDtypeStruct((height, depth), f32),
        ],
        in_specs=[spec],
        out_specs=[spec] * 3,
        scratch_shapes=[dma((CHUNKS,))] * 4
        + [dma((2 * CHUNKS,))] * 4
        + [dma((2,)), dma((2,)), dma((3,))],
        compiler_params=pltpu.CompilerParams(
            collective_id=0, has_side_effects=True, vmem_limit_bytes=32 * 2**20
        ),
        name="exchange",
    )(matrix)
    out, panel, pivot = pl.pallas_call(
        solve,
        out_shape=[
            jax.ShapeDtypeStruct((height, width), f32),
            jax.ShapeDtypeStruct((height // cols, depth), f32),
            jax.ShapeDtypeStruct((1, depth), f32),
        ],
        in_specs=[spec] * 4,
        out_specs=[spec] * 3,
        scratch_shapes=[VMEM((depth, depth), f32), VMEM((height, depth), f32)],
        compiler_params=pltpu.CompilerParams(vmem_limit_bytes=48 * 2**20),
        name="solve",
    )(matrix, col, diag, row)
    return out, panel, pivot.reshape(depth)


def solution(mesh):
    rows, cols = mesh.shape["prow"], mesh.shape["pcol"]
    return jax.shard_map(
        functools.partial(on_device, rows, cols),
        mesh=mesh,
        in_specs=(P("prow", "pcol"),),
        out_specs=(P("prow", "pcol"), P(("prow", "pcol"), None), P()),
        check_vma=False,
    )
```

```python
import functools

import jax
import jax.numpy as jnp
from jax import lax
from jax.experimental import pallas as pl
from jax.experimental.pallas import tpu as pltpu
from jax.sharding import PartitionSpec as P

NB = 256
PANELS = 2
BLOCK = 128
SUB = 8
CHUNKS = 8
ROW_CHUNKS = 4
DIAG_SLOT = (None, 0, 4, 8)
COL_SLOT = (1, 2, 3, 5, 6, 7, 9, 10)
ROW_SLOT = (1, 3, 5, 7)
SLOTS = 4

HIGHEST = lax.Precision.HIGHEST
MESH = pl.DeviceIdType.MESH
VMEM = pltpu.VMEM


def matmul(left, right):
    return lax.dot_general(
        left, right, (((1,), (0,)), ((), ())),
        precision=HIGHEST, preferred_element_type=jnp.float32,
    )


def against(left, right):
    return lax.dot_general(
        left, right, (((1,), (1,)), ((), ())),
        precision=HIGHEST, preferred_element_type=jnp.float32,
    )


def eliminate(block, pump):
    groups = BLOCK // SUB
    shape = (SUB, BLOCK)
    lane = lax.broadcasted_iota(jnp.int32, shape, 1)
    sub = lax.broadcasted_iota(jnp.int32, shape, 0)
    zero = jnp.zeros(shape, jnp.float32)
    rest = block
    done = []
    pivots = zero
    for v in range(groups):
        if v % (groups // SLOTS) == 0:
            pump(v // (groups // SLOTS))
        first = v * SUB
        own_rows, under = rest[:SUB], rest[SUB:]
        low = under.shape[0]
        wide = lambda x, t: jnp.broadcast_to(x[:, first + t : first + t + 1], x.shape)
        own = [wide(own_rows, t) for t in range(SUB)]
        inside = (lane >= first) & (lane < first + SUB)
        identity = jnp.where(lane == sub + first, 1.0, 0.0).astype(jnp.float32)
        own_rows = jnp.where(inside, identity, own_rows)
        if low:
            column = [wide(under, t) for t in range(SUB)]
            spot = lax.broadcasted_iota(jnp.int32, under.shape, 1)
            under = jnp.where((spot >= first) & (spot < first + SUB), 0.0, under)
        for t in range(SUB):
            pivot = jnp.broadcast_to(own[t][t : t + 1], shape)
            inverse = 1.0 / pivot
            pivots = jnp.where(lane == first + t, pivot, pivots)
            entries = {u: own[u][t : t + 1] for u in range(t + 1, SUB)}
            pivot_row = own_rows[t : t + 1]
            below = jnp.where(sub > t, own[t], zero)
            for u in range(t + 1, SUB):
                own[u] = own[u] - (below * entries[u]) * inverse
            own_rows = own_rows - (below * pivot_row) * inverse
            if low:
                weight = column[t] * inverse[0:1]
                for u in range(t + 1, SUB):
                    column[u] = column[u] - weight * entries[u]
                under = under - weight * pivot_row
        done.append(jnp.where(lane < first + SUB, own_rows, zero))
        rest = under
    return jnp.concatenate(done, axis=0), pivots[0:1, :]


def window(rows, cols, chain, a_ref, out_ref, panel_ref, pivot_ref,
           col_ref, diag_ref, row_ref, work, held, partner_ref, *sems):
    ds, dr, zs, zr, ys, yr, rs, rr, local = sems
    r, c = lax.axis_index("prow"), lax.axis_index("pcol")
    height, width = a_ref.shape
    depth = diag_ref.shape[0]
    count = depth // BLOCK
    piece = lax.rem(r, chain)
    other = chain - 1 - piece
    partner = r - piece + other
    has_next, has_prev = r + chain < rows, r >= chain
    even = lax.rem(c, 2) == 0
    mate = c + 1 - 2 * lax.rem(c, 2)
    has_right, has_left = even & (c + 2 < cols), even & (c >= 2)
    lead, gets = c == 0, c > 0

    barrier = pltpu.get_barrier_semaphore()

    def greet(dev):
        pl.semaphore_signal(barrier, inc=1, device_id=dev, device_id_type=MESH)

    greet((partner, c))
    greet((r, mate))
    pl.when(has_next)(lambda: greet((r + chain, c)))
    pl.when(has_prev)(lambda: greet((r - chain, c)))
    pl.when(has_right)(lambda: greet((r, c + 2)))
    pl.when(has_left)(lambda: greet((r, c - 2)))
    one = lambda flag: flag.astype(jnp.int32)
    pl.semaphore_wait(
        barrier, 2 + one(has_next) + one(has_prev) + one(has_right) + one(has_left)
    )

    def remote(source, target, send, recv, dev):
        return pltpu.make_async_remote_copy(
            src_ref=source, dst_ref=target, send_sem=send, recv_sem=recv,
            device_id=dev, device_id_type=MESH,
        )

    def strip(b):
        return diag_ref.at[b * BLOCK : (b + 1) * BLOCK, : (b + 1) * BLOCK]

    def own_strip(b):
        top = b * BLOCK % height
        return a_ref.at[top : top + BLOCK, : (b + 1) * BLOCK]

    def strip_copy(b, way, source):
        dev = ((r + chain, c), (partner, c), (r, c + 1), (r, c + 2))[way]
        return remote(source, strip(b), ds.at[way, b], dr.at[b], dev)

    def strip_routes(b):
        mine = lead & (piece == b * BLOCK // height)
        return ((0, mine & has_next), (1, mine), (3, has_right), (2, even))

    def owner_of(b):
        return lead & (r == b * BLOCK // height)

    def local_strip(b):
        return pltpu.make_async_copy(own_strip(b), strip(b), local.at[b])

    def move_strip(b):
        owner = owner_of(b)

        @pl.when(owner)
        def _():
            for way, flag in strip_routes(b):
                pl.when(flag)(lambda: strip_copy(b, way, own_strip(b)).start())
            local_strip(b).start()
            local_strip(b).wait()

        @pl.when(jnp.logical_not(owner))
        def _():
            strip_copy(b, 2, strip(b)).wait_recv()
            for way, flag in strip_routes(b):
                pl.when(flag)(lambda: strip_copy(b, way, strip(b)).start())

    step = height // CHUNKS

    def col_part(block, k):
        start = pl.multiple_of(block * height + k * step, step)
        return col_ref.at[pl.ds(start, step)]

    def z_copy(k, source):
        return remote(source, col_part(piece, k), zs.at[k], zr.at[k], (r + chain, c))

    def y_copy(k, block, source):
        return remote(source, col_part(block, k), ys.at[k], yr.at[k], (partner, c))

    def move_col(k):
        def send(source):
            pl.when(has_next)(lambda: z_copy(k, source).start())
            y_copy(k, piece, source).start()

        @pl.when(has_prev)
        def _():
            z_copy(k, col_part(piece, k)).wait_recv()
            send(col_part(piece, k))

        pl.when(jnp.logical_not(has_prev))(
            lambda: send(a_ref.at[k * step : (k + 1) * step])
        )

    row_step = height // ROW_CHUNKS

    def row_part(ref, k):
        return ref.at[k * row_step : (k + 1) * row_step]

    def row_copy(k, way, source):
        dev = ((r, c + 1), (r, c + 2))[way]
        return remote(source, row_part(row_ref, k), rs.at[way, k], rr.at[k], dev)

    def move_row(k):
        def send(source):
            pl.when(has_right)(lambda: row_copy(k, 1, source).start())
            pl.when(even)(lambda: row_copy(k, 0, source).start())

        @pl.when(gets)
        def _():
            row_copy(k, 0, row_part(row_ref, k)).wait_recv()
            send(row_part(row_ref, k))

        pl.when(lead)(lambda: send(row_part(a_ref, k)))

    def home_col():
        start = pl.multiple_of(piece * height, height)
        return pltpu.make_async_copy(a_ref, col_ref.at[pl.ds(start, height)], local.at[count])

    def home_row():
        return pltpu.make_async_copy(a_ref, row_ref, local.at[count + 1])

    def pump(slot):
        for b in range(1, count):
            if DIAG_SLOT[b] == slot:
                move_strip(b)
        for k in range(CHUNKS):
            if COL_SLOT[k] == slot:
                move_col(k)
        for k in range(ROW_CHUNKS):
            if ROW_SLOT[k] == slot:
                move_row(k)

    move_strip(0)
    pl.when(jnp.logical_not(has_prev))(lambda: home_col().start())
    pl.when(lead)(lambda: home_row().start())
    for b in range(count):
        here = slice(b * BLOCK, (b + 1) * BLOCK)
        before = slice(0, b * BLOCK)
        current = diag_ref[here, here]
        if b:
            factor = against(diag_ref[here, before], work[before, before])
            lower = factor / pivot_ref[:, before]
            current = current - against(lower, factor)
        inverse, pivots = eliminate(current, lambda q: pump(b * SLOTS + q))
        pivot_ref[:, here] = pivots
        work[here, here] = inverse
        if b:
            work[here, before] = -matmul(inverse, matmul(lower, work[before, before]))
        if b + 1 < count:
            work[here, (b + 1) * BLOCK :] = jnp.zeros(
                (BLOCK, depth - (b + 1) * BLOCK), jnp.float32
            )

    pl.when(jnp.logical_not(has_prev))(lambda: home_col().wait())
    pl.when(lead)(lambda: home_row().wait())
    for k in range(CHUNKS):
        y_copy(k, other, col_part(other, k)).wait_recv()

    for b in range(count):
        here = slice(b * BLOCK, (b + 1) * BLOCK)
        upto = slice(0, (b + 1) * BLOCK)
        factor = against(row_ref[:, upto], work[here, upto])
        grow = r * height + lax.broadcasted_iota(jnp.int32, factor.shape, 0)
        held[:, here] = jnp.where(grow >= b * BLOCK // NB * NB, factor, 0.0)
        partner_ref[here, :] = matmul(work[here, upto], col_ref[upto, :])
    weighed = held[...] / pivot_ref[...]
    update = a_ref[...] - matmul(weighed, partner_ref[...])
    grow = r * height + lax.broadcasted_iota(jnp.int32, update.shape, 0)
    gcol = c * width + lax.broadcasted_iota(jnp.int32, update.shape, 1)
    out_ref[...] = jnp.where((grow >= depth) & (gcol >= depth), update, 0.0)
    portion = panel_ref.shape[0]
    panel_ref[...] = held[pl.ds(pl.multiple_of(c * portion, portion), portion), :]

    for b in range(count):
        for way, flag in strip_routes(b):
            pl.when(flag)(lambda: strip_copy(b, way, strip(b)).wait_send())
    for k in range(CHUNKS):
        pl.when(has_next)(lambda: z_copy(k, col_part(piece, k)).wait_send())
        y_copy(k, piece, col_part(piece, k)).wait_send()
    for k in range(ROW_CHUNKS):
        pl.when(has_right)(lambda: row_copy(k, 1, row_part(row_ref, k)).wait_send())
        pl.when(even)(lambda: row_copy(k, 0, row_part(row_ref, k)).wait_send())


def on_device(rows, cols, matrix):
    height, width = matrix.shape
    depth = NB * PANELS
    chain = depth // height
    count = depth // BLOCK
    f32 = jnp.float32
    spec = pl.BlockSpec(memory_space=VMEM)
    dma = pltpu.SemaphoreType.DMA
    out, panel, pivot = pl.pallas_call(
        functools.partial(window, rows, cols, chain),
        out_shape=[
            jax.ShapeDtypeStruct((height, width), f32),
            jax.ShapeDtypeStruct((height // cols, depth), f32),
            jax.ShapeDtypeStruct((1, depth), f32),
        ],
        in_specs=[spec],
        out_specs=[spec] * 3,
        scratch_shapes=[
            VMEM((depth, width), f32),
            VMEM((depth, depth), f32),
            VMEM((height, depth), f32),
            VMEM((depth, depth), f32),
            VMEM((height, depth), f32),
            VMEM((depth, width), f32),
            dma((4, count)),
            dma((count,)),
            dma((CHUNKS,)),
            dma((CHUNKS,)),
            dma((CHUNKS,)),
            dma((CHUNKS,)),
            dma((2, ROW_CHUNKS)),
            dma((ROW_CHUNKS,)),
            dma((count + 2,)),
        ],
        compiler_params=pltpu.CompilerParams(
            collective_id=0, has_side_effects=True, vmem_limit_bytes=48 * 2**20
        ),
        name="window",
    )(matrix)
    return out, panel, pivot.reshape(depth)


def solution(mesh):
    rows, cols = mesh.shape["prow"], mesh.shape["pcol"]
    return jax.shard_map(
        functools.partial(on_device, rows, cols),
        mesh=mesh,
        in_specs=(P("prow", "pcol"),),
        out_specs=(P("prow", "pcol"), P(("prow", "pcol"), None), P()),
        check_vma=False,
    )
```

```python
import functools

import jax
import jax.numpy as jnp
from jax import lax
from jax.experimental import pallas as pl
from jax.experimental.pallas import tpu as pltpu
from jax.sharding import PartitionSpec as P

NB = 256
PANELS = 2
BLOCK = 128
SUB = 8
CHUNKS = 8
LAG = 3

HIGHEST = lax.Precision.HIGHEST
MESH = pl.DeviceIdType.MESH
VMEM = pltpu.VMEM


def matmul(left, right):
    return lax.dot_general(
        left, right, (((1,), (0,)), ((), ())),
        precision=HIGHEST, preferred_element_type=jnp.float32,
    )


def against(left, right):
    return lax.dot_general(
        left, right, (((1,), (1,)), ((), ())),
        precision=HIGHEST, preferred_element_type=jnp.float32,
    )


def exchange(rows, cols, chain, a_ref, col_ref, diag_ref, row_ref, *sems):
    zs, zr, ys, yr, es, er, fs, fr, rs, rr, local = sems
    r, c = lax.axis_index("prow"), lax.axis_index("pcol")
    height = a_ref.shape[0]
    piece = lax.rem(r, chain)
    other = chain - 1 - piece
    partner = r - piece + other
    step = height // CHUNKS
    has_next, has_prev = r + chain < rows, r >= chain
    even = lax.rem(c, 2) == 0
    mate = c + 1 - 2 * lax.rem(c, 2)
    has_right, has_left = even & (c + 2 < cols), even & (c >= 2)
    gets = c > 0

    barrier = pltpu.get_barrier_semaphore()

    def greet(dev):
        pl.semaphore_signal(barrier, inc=1, device_id=dev, device_id_type=MESH)

    greet((partner, c))
    greet((r, mate))
    pl.when(has_next)(lambda: greet((r + chain, c)))
    pl.when(has_prev)(lambda: greet((r - chain, c)))
    pl.when(has_right)(lambda: greet((r, c + 2)))
    pl.when(has_left)(lambda: greet((r, c - 2)))
    one = lambda flag: flag.astype(jnp.int32)
    pl.semaphore_wait(
        barrier, 2 + one(has_next) + one(has_prev) + one(has_right) + one(has_left)
    )

    def remote(ref, source, target, send, recv, dev):
        return pltpu.make_async_remote_copy(
            src_ref=source, dst_ref=ref.at[target] if target is not None else ref,
            send_sem=send, recv_sem=recv, device_id=dev, device_id_type=MESH,
        )

    def part(block, k):
        return pl.ds(pl.multiple_of(block * height + k * step, step), step)

    def z_copy(k):
        s = part(piece, k)
        return remote(col_ref, col_ref.at[s], s, zs.at[k], zr.at[k], (r + chain, c))

    def y_copy(k, block):
        s = part(block, k)
        return remote(col_ref, col_ref.at[s], s, ys.at[k], yr.at[k], (partner, c))

    def mate_copy(source, block, k, q):
        s = part(block, k)
        return remote(diag_ref, source.at[s], s, es.at[q], er.at[q], (r, c + 1))

    def right_copy(source, block, k, q):
        s = part(block, k)
        return remote(diag_ref, source.at[s], s, fs.at[q], er.at[q], (r, c + 2))

    def row_mate(source):
        return remote(row_ref, source, None, rs.at[0], rr.at[0], (r, c + 1))

    def row_right(source):
        return remote(row_ref, source, None, rs.at[1], rr.at[0], (r, c + 2))

    @pl.when(jnp.logical_not(has_prev))
    def _():
        copy = pltpu.make_async_copy(
            a_ref, col_ref.at[pl.ds(pl.multiple_of(piece * height, height), height)], local.at[0]
        )
        copy.start()
        copy.wait()

    def spread(source, block, k, q):
        pl.when(even)(lambda: mate_copy(source, block, k, q).start())
        pl.when(has_right)(lambda: right_copy(source, block, k, q).start())

    def take_row():
        row_mate(row_ref).wait_recv()

        @pl.when(even)
        def _():
            pl.when(has_right)(lambda: row_right(row_ref).start())
            row_mate(row_ref).start()

    def take(k):
        for block, n, q in ((piece, k, k), (other, k - 1, CHUNKS + k - 1)):
            if 0 <= n < CHUNKS:
                mate_copy(diag_ref, block, n, q).wait_recv()
                pl.when(even)(lambda: spread(diag_ref, block, n, q))

    home = pltpu.make_async_copy(a_ref, row_ref, local.at[1])

    @pl.when(c == 0)
    def _():
        pl.when(has_right)(lambda: row_right(a_ref).start())
        row_mate(a_ref).start()
        home.start()

    for k in range(CHUNKS):
        pl.when(has_prev)(lambda: z_copy(k).wait_recv())
        pl.when(has_next)(lambda: z_copy(k).start())
        y_copy(k, piece).start()
        pl.when(c == 0)(lambda: spread(col_ref, piece, k, k))
        if k >= 1:
            y_copy(k - 1, other).wait_recv()
            pl.when(c == 0)(lambda: spread(col_ref, other, k - 1, CHUNKS + k - 1))
        if k == LAG:
            pl.when(gets)(take_row)
        if k > LAG:
            pl.when(gets)(lambda: take(k - LAG - 1))

    k = CHUNKS - 1
    y_copy(k, other).wait_recv()

    @pl.when(c == 0)
    def _():
        spread(col_ref, other, k, CHUNKS + k)
        copy = pltpu.make_async_copy(col_ref, diag_ref, local.at[2])
        copy.start()
        copy.wait()
        home.wait()

    @pl.when(gets)
    def _():
        for k in range(CHUNKS - LAG - 1, CHUNKS + 1):
            take(k)

    for k in range(CHUNKS):
        pl.when(has_next)(lambda: z_copy(k).wait_send())
        y_copy(k, piece).wait_send()
    for q in range(2 * CHUNKS):
        block, k = (piece, q) if q < CHUNKS else (other, q - CHUNKS)
        pl.when(even)(lambda: mate_copy(diag_ref, block, k, q).wait_send())
        pl.when(has_right)(lambda: right_copy(diag_ref, block, k, q).wait_send())
    pl.when(even)(lambda: row_mate(row_ref).wait_send())
    pl.when(has_right)(lambda: row_right(row_ref).wait_send())


def eliminate(block):
    groups = BLOCK // SUB
    shape = (SUB, BLOCK)
    lane = lax.broadcasted_iota(jnp.int32, shape, 1)
    sub = lax.broadcasted_iota(jnp.int32, shape, 0)
    zero = jnp.zeros(shape, jnp.float32)
    rows = [block[w * SUB : (w + 1) * SUB, :] for w in range(groups)]
    pivots = zero
    spread = lambda x, t: jnp.broadcast_to(x[t : t + 1, :], shape)
    for v in range(groups):
        first = v * SUB
        column = {
            w: [
                jnp.broadcast_to(rows[w][:, first + t : first + t + 1], shape)
                for t in range(SUB)
            ]
            for w in range(v, groups)
        }
        inside = (lane >= first) & (lane < first + SUB)
        identity = jnp.where(lane == sub + first, 1.0, 0.0).astype(jnp.float32)
        rows[v] = jnp.where(inside, identity, rows[v])
        for w in range(v + 1, groups):
            rows[w] = jnp.where(inside, zero, rows[w])
        for t in range(SUB):
            own = column[v]
            pivot = spread(own[t], t)
            inverse = 1.0 / pivot
            pivots = jnp.where(lane == first + t, pivot, pivots)
            entries = {u: spread(own[u], t) for u in range(t + 1, SUB)}
            pivot_row = spread(rows[v], t)
            below = jnp.where(sub > t, own[t], zero)
            for u in range(t + 1, SUB):
                own[u] = own[u] - (below * entries[u]) * inverse
            rows[v] = rows[v] - (below * pivot_row) * inverse
            for w in range(v + 1, groups):
                weight = column[w][t] * inverse
                for u in range(t + 1, SUB):
                    column[w][u] = column[w][u] - weight * entries[u]
                rows[w] = rows[w] - weight * pivot_row
        rows[v] = jnp.where(lane < first + SUB, rows[v], zero)
    return jnp.concatenate(rows, axis=0), pivots[0:1, :]


def solve(a_ref, col_ref, diag_ref, row_ref, out_ref, panel_ref, pivot_ref, work, held):
    r, c = lax.axis_index("prow"), lax.axis_index("pcol")
    depth = diag_ref.shape[0]
    height, width = a_ref.shape
    count = depth // BLOCK
    work[...] = diag_ref[...]
    for b in range(count):
        here = slice(b * BLOCK, (b + 1) * BLOCK)
        inverse, pivots = eliminate(work[here, here])
        pivot_ref[:, here] = pivots
        if b:
            left = matmul(inverse, work[here, : b * BLOCK])
            work[here, : b * BLOCK] = left
        if b + 1 < count:
            after = slice((b + 1) * BLOCK, depth)
            right = matmul(inverse, work[here, after])
            lower = against(work[after, here], inverse) / pivots
            work[after, after] = work[after, after] - matmul(lower, right)
            if b:
                work[after, : b * BLOCK] = work[after, : b * BLOCK] - matmul(lower, left)
            work[after, here] = -matmul(lower, inverse)
        work[here, here] = inverse
        if b + 1 < count:
            work[here, after] = jnp.zeros((BLOCK, depth - (b + 1) * BLOCK), jnp.float32)
    factor = against(row_ref[...], work[...])
    partner = matmul(work[...], col_ref[...])
    weighed = factor / pivot_ref[...]
    update = a_ref[...] - matmul(weighed, partner)
    grow = r * height + lax.broadcasted_iota(jnp.int32, update.shape, 0)
    gcol = c * width + lax.broadcasted_iota(jnp.int32, update.shape, 1)
    out_ref[...] = jnp.where((grow >= depth) & (gcol >= depth), update, 0.0)
    grow = r * height + lax.broadcasted_iota(jnp.int32, factor.shape, 0)
    panel = lax.broadcasted_iota(jnp.int32, factor.shape, 1) // NB
    held[...] = jnp.where(grow >= panel * NB, factor, 0.0)
    portion = panel_ref.shape[0]
    panel_ref[...] = held[pl.ds(pl.multiple_of(c * portion, portion), portion), :]


def on_device(rows, cols, matrix):
    height, width = matrix.shape
    depth = NB * PANELS
    chain = depth // height
    f32 = jnp.float32
    spec = pl.BlockSpec(memory_space=VMEM)
    dma = pltpu.SemaphoreType.DMA
    col, diag, row = pl.pallas_call(
        functools.partial(exchange, rows, cols, chain),
        out_shape=[
            jax.ShapeDtypeStruct((depth, width), f32),
            jax.ShapeDtypeStruct((depth, depth), f32),
            jax.ShapeDtypeStruct((height, depth), f32),
        ],
        in_specs=[spec],
        out_specs=[spec] * 3,
        scratch_shapes=[dma((CHUNKS,))] * 4
        + [dma((2 * CHUNKS,))] * 4
        + [dma((2,)), dma((2,)), dma((3,))],
        compiler_params=pltpu.CompilerParams(
            collective_id=0, has_side_effects=True, vmem_limit_bytes=32 * 2**20
        ),
        name="exchange",
    )(matrix)
    out, panel, pivot = pl.pallas_call(
        solve,
        out_shape=[
            jax.ShapeDtypeStruct((height, width), f32),
            jax.ShapeDtypeStruct((height // cols, depth), f32),
            jax.ShapeDtypeStruct((1, depth), f32),
        ],
        in_specs=[spec] * 4,
        out_specs=[spec] * 3,
        scratch_shapes=[VMEM((depth, depth), f32), VMEM((height, depth), f32)],
        compiler_params=pltpu.CompilerParams(vmem_limit_bytes=48 * 2**20),
        name="solve",
    )(matrix, col, diag, row)
    return out, panel, pivot.reshape(depth)


def solution(mesh):
    rows, cols = mesh.shape["prow"], mesh.shape["pcol"]
    return jax.shard_map(
        functools.partial(on_device, rows, cols),
        mesh=mesh,
        in_specs=(P("prow", "pcol"),),
        out_specs=(P("prow", "pcol"), P(("prow", "pcol"), None), P()),
        check_vma=False,
    )
```
